32 devices in a mesh: energy: 4 (over z), views: 8 (over y, x, core).
Axes of the slice: x: 2, y: 2, z: 4, core: 2. Of those that a mesh axis runs over, the one named last changes fastest.
Arguments:
- projector_tiles: float32 [32, 48, 128, 256], P('views'), may hold values from -0.0546875 to 0.0546875
- tile_blocks: int32 [32, 48], P('views'), may hold values from 0 to 63
- ray_counts: int32 [32], P('views'), may hold values from 64 to 128
- sinogram: float32 [64, 4096], P('energy', 'views'), may hold values from -6 to 6
- ray_weights: float32 [64, 4096], P('energy', 'views'), may hold values from 0.25 to 4
- start_volume: float32 [64, 16384], P('energy', 'views'), may hold values from -6 to 6
- split_target: float32 [8, 64, 2048], P('views', None, 'energy'), may hold values from -6 to 6
- scaled_dual: float32 [8, 64, 2048], P('views', None, 'energy'), may hold values from -3 to 3
Outputs:
- new_volume: float32 [64, 16384], P('energy', 'views')
- new_split: float32 [8, 64, 2048], P('views', None, 'energy')
- new_dual: float32 [8, 64, 2048], P('views', None, 'energy')
The draws below stay inside these ranges and needn't reach their ends.
Inputs may be any that keep to these rules, and one draw needn't show every extreme that they name: `tile_blocks`: block indices may repeat within a ray block. `ray_counts`: rays of a block at or past its count are padding.
All inputs are finite; a program needn't handle non-finite values.
Results may differ from the reference program's by a relative error of at most 0.00022.
Values sent between devices are 32-bit elements; how exact they have to be, the bound alone decides.
No kernel may reach another device: no remote copies, remote signals or barrier semaphores. Data moves between devices by JAX's collectives and lax.ppermute only.
A program may use at most 128 MiB of HBM per device.

```python
import math
import jax
import jax.numpy as jnp
from jax import lax

C = 64
PV = 64
RB_DEV = 4
RT = 128
VB = 256
TPR = 48
ITERS = 3
SEG = 2048
VOX = 16384
NB = 64
RAYS = 4096
N_VIEWS = 8


def place_ends(entries, key, smallest, high):
    dims = entries.shape
    place = [jax.random.randint(jax.random.fold_in(key, axis), (), 0, dims[axis]) for axis in range(len(dims))]
    entries = entries.at[tuple(place)].set(smallest)
    longest = dims.index(max(dims))
    place[longest] = (place[longest] + 1) % dims[longest]
    return entries.at[tuple(place)].set(high)


def level_of(stream_key, dims, shards, least, largest):
    def one(position, parts):
        steps = jax.random.uniform(jax.random.fold_in(jax.random.fold_in(stream_key, 6), position), (parts,), jnp.float32, least / len(shards), largest / len(shards))
        return jnp.repeat(jnp.exp(steps), dims[position] // parts).reshape((-1,) + (1,) * (len(dims) - position - 1))

    loudness = one(*shards[0])
    for cut in shards[1:]:
        loudness = loudness * one(*cut)
    return loudness


def normal_values(rng, shape, width, limit, pieces=(), kind=jnp.bfloat16):
    drawn = width * jax.random.normal(rng, shape, jnp.float32)
    if pieces:
        drawn = drawn * level_of(rng, shape, pieces, -0.22, 0.18)
    return jnp.clip(drawn, -limit, limit).astype(kind)


def setup_inputs(seed: int = 0) -> dict:
    seeds = jax.random.split(jax.random.key(seed), 9)
    return {
        "projector_tiles": normal_values(seeds[0], (N_VIEWS * RB_DEV, TPR, RT, VB), (TPR * VB) ** -0.5, 0.0546875, ((0, 8),), jnp.float32),
        "tile_blocks": place_ends(jax.random.randint(seeds[1], (N_VIEWS * RB_DEV, TPR), 0, NB), jax.random.fold_in(seeds[1], 1), 0, NB - 1).astype(jnp.int32),
        "ray_counts": place_ends(jax.random.randint(seeds[2], (N_VIEWS * RB_DEV,), RT // 2, RT + 1), jax.random.fold_in(seeds[2], 1), RT // 2, RT).astype(jnp.int32),
        "sinogram": normal_values(seeds[3], (C, RAYS), 1.0, 6.0, ((0, 4), (1, 8)), jnp.float32),
        "ray_weights": jnp.clip(jnp.exp(math.log(4.0) - 2.7725887 * jax.random.uniform(seeds[4], (C, RAYS), jnp.float32) ** level_of(seeds[4], (C, RAYS), ((0, 4), (1, 8)), -0.2, 0.2)), 0.25, 4.0),
        "start_volume": normal_values(seeds[5], (C, VOX), 1.0, 6.0, ((0, 4), (1, 8)), jnp.float32),
        "split_target": normal_values(seeds[6], (N_VIEWS, C, SEG), 1.0, 6.0, ((0, 8), (2, 4)), jnp.float32),
        "scaled_dual": normal_values(seeds[7], (N_VIEWS, C, SEG), 0.5, 3.0, ((0, 8), (2, 4)), jnp.float32),
    }


PENALTY = 1.0
SHRINK = 16.0
exact_mode = lax.Precision.HIGHEST

def forward_all(volume, projector_tiles, tile_blocks):
    channel_count = volume.shape[0]
    block_voxels = projector_tiles.shape[3]
    block_grid = volume.reshape(channel_count, -1, block_voxels)

    def one_block(pair):
        tiles_here, blocks_here = pair
        columns = block_grid[:, blocks_here]
        return jnp.einsum('ctv,tkv->ck', columns, tiles_here, precision=exact_mode)
    projected = lax.map(one_block, (projector_tiles, tile_blocks))
    return jnp.transpose(projected, (1, 0, 2)).reshape(channel_count, -1)

def backward_all(weighted, projector_tiles, tile_blocks, voxel_count):
    channel_count = weighted.shape[0]
    ray_blocks, per_block, ray_length, block_voxels = projector_tiles.shape
    ray_parts = jnp.transpose(weighted.reshape(channel_count, ray_blocks, ray_length), (1, 0, 2))

    def add_block(block_grid, triple):
        tiles_here, blocks_here, rays_here = triple
        spread_rays = jnp.einsum('ck,tkv->ctv', rays_here, tiles_here, precision=exact_mode)
        return (block_grid.at[:, blocks_here].add(spread_rays), None)
    start_grid = jnp.zeros((channel_count, voxel_count // block_voxels, block_voxels), jnp.float32)
    block_grid, unused_out = lax.scan(add_block, start_grid, (projector_tiles, tile_blocks, ray_parts))
    return block_grid.reshape(channel_count, voxel_count)

def to_volume(patched):
    return jnp.transpose(patched, (1, 0, 2)).reshape(patched.shape[1], -1)

def to_patched(volume, view_count):
    return jnp.transpose(volume.reshape(volume.shape[0], view_count, -1), (1, 0, 2))

def shrink_patches(patched):
    view_count, channel_count, segment_len = patched.shape
    blocks = patched.reshape(view_count, channel_count, segment_len // PV, PV)
    gram_matrix = jnp.einsum('acpv,adpv->apcd', blocks, blocks, precision=exact_mode)
    shifted = gram_matrix + SHRINK * jnp.eye(channel_count, dtype=jnp.float32)
    factor = jnp.linalg.cholesky(shifted)
    right_side = jnp.transpose(blocks, (0, 2, 1, 3))
    solved = jax.scipy.linalg.cho_solve((factor, True), right_side)
    shrunk = right_side - SHRINK * solved
    return jnp.transpose(shrunk, (0, 2, 1, 3)).reshape(view_count, channel_count, segment_len)

def reference(projector_tiles, tile_blocks, ray_counts, sinogram, ray_weights, start_volume, split_target, scaled_dual):
    ray_length = projector_tiles.shape[2]
    live_rays = (lax.broadcasted_iota(jnp.int32, (ray_counts.shape[0], ray_length), 1) < ray_counts[:, None]).astype(jnp.float32)
    ray_scale = ray_weights * live_rays.reshape(1, -1)
    voxel_count = start_volume.shape[1]
    target = to_volume(split_target - scaled_dual)

    def normal_map(vector, measured, anchor):
        weighted = ray_scale * (measured - forward_all(vector, projector_tiles, tile_blocks))
        return backward_all(weighted, projector_tiles, tile_blocks, voxel_count) + PENALTY * (anchor - vector)
    residual = normal_map(start_volume, sinogram, target)
    direction = residual
    volume_now = start_volume
    norm_now = jnp.sum(jnp.square(residual), axis=1)
    for iteration in range(ITERS):
        mapped = -normal_map(direction, 0.0, 0.0)
        step_size = (norm_now / jnp.sum(direction * mapped, axis=1))[:, None]
        volume_now = volume_now + step_size * direction
        residual = residual - step_size * mapped
        norm_next = jnp.sum(jnp.square(residual), axis=1)
        direction = residual + (norm_next / norm_now)[:, None] * direction
        norm_now = norm_next
    volume_patch = to_patched(volume_now, split_target.shape[0])
    new_split = shrink_patches(volume_patch + scaled_dual)
    new_dual = scaled_dual + volume_patch - new_split
    return (volume_now, new_split, new_dual)
```

```python
import functools

import jax
import jax.numpy as jnp
from jax import lax
from jax.experimental import pallas as pl
from jax.experimental.pallas import tpu as pltpu
from jax.sharding import PartitionSpec as P

PV = 64
ITERS = 3
PENALTY = 1.0
SHRINK = 16.0
LANES = 128
LOOPED = ("first", "mid")
PIVOTS = 2
F32, BF16 = jnp.float32, jnp.bfloat16

VM = pl.BlockSpec(memory_space=pltpu.VMEM)
SM = pl.BlockSpec(memory_space=pltpu.SMEM)
ANY = pl.BlockSpec(memory_space=pl.ANY)
MIB = 1 << 20


def sds(shape, dtype=F32):
    return jax.ShapeDtypeStruct(shape, dtype)


def call(body, outs, ins, specs, scratch=(), limit=12, flops=0, moved=0, out_specs=None, name=None):
    return pl.pallas_call(
        body,
        out_shape=outs,
        in_specs=specs,
        out_specs=out_specs if out_specs is not None else jax.tree.map(lambda _: VM, outs),
        scratch_shapes=list(scratch),
        compiler_params=pltpu.CompilerParams(vmem_limit_bytes=limit * MIB),
        cost_estimate=pl.CostEstimate(flops=flops, bytes_accessed=moved, transcendentals=0),
        name=name,
    )(*ins)


def halves(x):
    hi = x.astype(BF16).astype(F32)
    return hi, x - hi


def prepare(tiles, ids, step, depth=6):
    R, T, rays, width = tiles.shape
    per = T // step
    trips = R * per

    def body(ids_ref, src, out, token, buf, sem):
        token[...] = jnp.zeros_like(token)

        def copy(i):
            slot = lax.rem(i, depth)
            at = lax.rem(i, per) * step
            return pltpu.make_async_copy(src.at[i // per, pl.ds(at, step)], buf.at[slot], sem.at[slot])

        for a in range(depth - 1):
            copy(a).start()

        def trip(i, carry):
            @pl.when(i + depth - 1 < trips)
            def _():
                copy(i + depth - 1).start()

            copy(i).wait()
            slot = lax.rem(i, depth)
            r, base = i // per, lax.rem(i, per) * step
            for a in range(step):
                hi, lo = halves(buf[slot, a])
                at = pl.multiple_of((base + a) * width, width)
                out[r, :rays, pl.ds(at, width)] = hi.astype(BF16)
                out[r, rays:, pl.ds(at, width)] = lo.astype(BF16)
            return carry

        lax.fori_loop(0, trips, trip, 0)

    return call(
        body,
        [pltpu.VMEM((R, 2 * rays, T * width), BF16), sds((8, LANES))],
        (ids, tiles),
        [SM, ANY],
        [pltpu.VMEM((depth, step, rays, width), F32), pltpu.SemaphoreType.DMA((depth,))],
        moved=tiles.size * 8,
        flops=tiles.size * 4,
        name="prepare",
    )


def apply_body(mode, dims, refs):
    n, C, seg, R, T, rays, vb = dims
    nb = seg // vb
    ext = LANES if mode != "first" else 0
    it = iter(refs)
    me_ref, blocks = next(it), next(it)
    pieces = [next(it) for _ in range(n)]
    tt, scale_ref = next(it), next(it)
    if mode == "first":
        sino, _ = next(it), next(it)
    if mode in ("mid", "last"):
        d_prev, ad_prev, rr_prev = next(it), next(it), next(it)
    if mode != "last":
        keep = [next(it) for _ in range(n // 2)]
        send = [next(it) for _ in range(n // 2)]
    if mode == "last":
        scal_out = next(it)
    if mode != "first":
        d_out, rr_out = next(it), next(it)
    if mode in ("zero", "mid"):
        ad_out = next(it)
    vs = next(it)
    weighted = next(it)
    columns = next(it)
    acc = next(it) if mode != "last" else None
    me = me_ref[0]

    for i in range(n):
        dev = me ^ i
        for j in range(nb):
            hi, lo = halves(pieces[i][:, j * vb : (j + 1) * vb])
            vs[dev * nb + j] = jnp.concatenate([hi, lo], axis=0).astype(BF16)

    partial = jnp.zeros((C, LANES), F32)
    beta = None
    if mode != "first":
        parts = pieces[0][:, seg:]
        for i in range(1, n):
            parts = parts + pieces[i][:, seg:]
        rr = jnp.sum(parts, axis=1, keepdims=True)
        rr_out[...] = jnp.broadcast_to(rr, (C, LANES))
        d = pieces[0][:, :seg]
        if mode != "zero":
            beta = rr / rr_prev[:, :1]
            d = d + beta * d_prev[...]
        d_out[...] = d
        squares = d * d
        for j in range(seg // LANES):
            partial = partial + squares[:, j * LANES : (j + 1) * LANES]

    for r in range(R):
        for t in range(T):
            columns[:, t * vb : (t + 1) * vb] = vs[blocks[r, t]]
        total = lax.dot_general(
            tt[r], columns[...], (((1,), (1,)), ((), ())), preferred_element_type=F32
        ).T
        both = total[:C] + total[C:]
        ray = both[:, :rays] + both[:, rays:]
        here = slice(r * rays, (r + 1) * rays)
        scale = scale_ref[:, here]
        if mode == "first":
            weight = scale * (sino[:, here] - ray)
        else:
            if mode != "zero":
                ray = ray + beta * ad_prev[:, here]
            if mode != "last":
                ad_out[:, here] = ray
            weight = scale * ray
            product = weight * ray
            for j in range(rays // LANES):
                partial = partial + product[:, j * LANES : (j + 1) * LANES]
        if mode != "last":
            hi, lo = halves(weight)
            stacked = jnp.concatenate([hi, lo], axis=0)
            weighted[r] = jnp.concatenate([stacked, stacked], axis=1).astype(BF16)
    if mode == "last":
        scal_out[...] = partial
        return

    acc[...] = jnp.zeros_like(acc)
    def back(r, carry):
        lhs = weighted[r]

        for t in range(T):
            out = lax.dot_general(
                lhs, tt[r, :, t * vb : (t + 1) * vb], (((1,), (0,)), ((), ())), preferred_element_type=F32
            )
            b = blocks[r, t]
            acc[b] = acc[b] + (out[:C] + out[C:])
        return carry

    if mode in LOOPED:
        lax.fori_loop(0, R, back, 0)
    else:
        for r in range(R):
            back(r, 0)

    for j in range(n // 2):
        for dest, out in ((me ^ (2 * j), keep[j]), (me ^ (2 * j + 1), send[j])):
            for q in range(nb):
                out[:, q * vb : (q + 1) * vb] = acc[dest * nb + q]
            if ext:
                out[:, seg:] = partial


def apply(mode, dims, *ins):
    n, C, seg, R, T, rays, vb = dims
    ext = LANES if mode != "first" else 0
    outs = []
    if mode != "last":
        outs += [sds((C, seg + ext))] * n
    else:
        outs += [sds((C, LANES))]
    if mode != "first":
        outs += [sds((C, seg)), sds((C, LANES))]
    if mode in ("zero", "mid"):
        outs += [sds((C, R * rays))]
    scratch = [
        pltpu.VMEM((n * (seg // vb), 2 * C, vb), BF16),
        pltpu.VMEM((R, 2 * C, 2 * rays), BF16),
        pltpu.VMEM((2 * C, T * vb), BF16),
    ]
    if mode != "last":
        scratch.append(pltpu.VMEM((n * (seg // vb), C, vb), F32))
    specs = [SM, SM] + [VM] * (len(ins) - 2)
    return call(
        lambda *refs: apply_body(mode, dims, refs),
        outs,
        ins,
        specs,
        scratch,
        flops=4 * C * R * T * rays * vb,
        moved=R * T * rays * vb * 4,
        name="apply_" + mode,
    )


def fold(x):
    total = x[:, :LANES]
    for j in range(1, x.shape[1] // LANES):
        total = total + x[:, j * LANES : (j + 1) * LANES]
    return total


def update_first(parts, volume, target):
    C, seg = volume.shape

    def body(*refs):
        got = refs[: len(parts)]
        vol, tgt, out = refs[len(parts) :]
        total = got[0][...]
        for g in got[1:]:
            total = total + g[...]
        r = total + PENALTY * (tgt[...] - vol[...])
        out[:, :seg] = r
        out[:, seg:] = fold(r * r)

    return call(body, sds((C, seg + LANES)), (*parts, volume, target), [VM] * (len(parts) + 2), name="update_first")


def update(parts, volume, residual, direction, rr):
    C, seg = volume.shape

    def body(*refs):
        got = refs[: len(parts)]
        vol, res, dirn, rr_ref, vol_out, out = refs[len(parts) :]
        total = got[0][...]
        for g in got[1:]:
            total = total + g[...]
        d = dirn[...]
        alpha = rr_ref[:, :1] / jnp.sum(total[:, seg:], axis=1, keepdims=True)
        vol_out[...] = vol[...] + alpha * d
        r = res[:, :seg] - alpha * (total[:, :seg] + PENALTY * d)
        out[:, :seg] = r
        out[:, seg:] = fold(r * r)

    return call(
        body,
        [sds((C, seg)), sds((C, seg + LANES))],
        (*parts, volume, residual, direction, rr),
        [VM] * (len(parts) + 4),
        name="update",
    )


def finish(parts, volume, direction, rr, group, E):
    C, seg = volume.shape
    width = seg // E

    def body(*refs):
        e_ref, got = refs[0], refs[1 : 1 + len(parts)]
        vol, dirn, rr_ref, vol_out = refs[1 + len(parts) : 5 + len(parts)]
        outs = refs[5 + len(parts) :]
        total = got[0][...]
        for g in got[1:]:
            total = total + g[...]
        alpha = rr_ref[:, :1] / jnp.sum(total, axis=1, keepdims=True)
        vol_out[...] = vol[...] + alpha * dirn[...]
        for k in range(E):
            at = pl.multiple_of((e_ref[1] ^ k) * width, LANES)
            outs[k][...] = vol_out[:, pl.ds(at, width)]

    got = call(
        body,
        [sds((C, seg))] + [sds((C, width))] * E,
        (group, *parts, volume, direction, rr),
        [SM] + [VM] * (len(parts) + 3),
        name="finish",
    )
    return got[0], got[1:]


def split_target_pieces(split_target, scaled_dual, group, E):
    full, width = split_target.shape
    C = full // E

    def body(e_ref, st, sd, *outs):
        for k in range(E):
            at = pl.multiple_of((e_ref[1] ^ k) * C, 8)
            outs[k][...] = st[pl.ds(at, C), :] - sd[pl.ds(at, C), :]

    return call(body, [sds((C, width))] * E, (group, split_target, scaled_dual), [SM, VM, VM], name="target_pieces")


def join_target(pieces, group):
    E = len(pieces)
    C, width = pieces[0].shape

    def body(e_ref, *refs):
        for k in range(E):
            at = pl.multiple_of((e_ref[1] ^ k) * width, LANES)
            refs[E][:, pl.ds(at, width)] = refs[k][...]

    return call(body, sds((C, width * E)), (group, *pieces), [SM] + [VM] * E, name="join_target")


def shrink(pieces, scaled_dual, group):
    E = len(pieces)
    C, width = pieces[0].shape
    N = C * E
    patches = width // PV

    def body(e_ref, *refs):
        got, sd = refs[:E], refs[E]
        split_out, dual_out, vol, aug, rows, solved = refs[E + 1 :]
        for k in range(E):
            at = pl.multiple_of((e_ref[1] ^ k) * C, 8)
            vol[pl.ds(at, C), :] = got[k][...]
        lane = lax.broadcasted_iota(jnp.int32, (N, 2 * PV), 1)
        left = lane < PV
        diag = jnp.where(lane == lax.broadcasted_iota(jnp.int32, (N, 2 * PV), 0), F32(SHRINK), F32(0))
        for q in range(patches // 2):
            here = slice(q * 2 * PV, (q + 1) * 2 * PV)
            pair = vol[:, here] + sd[:, here]
            turned = pltpu.roll(pair, PV, 1)
            for h, (first, other) in enumerate(((pair, turned), (turned, pair))):
                only = jnp.where(left, first, 0.0)
                gram = lax.dot_general(
                    only, jnp.concatenate([first, first], axis=0), (((1,), (1,)), ((), ())),
                    precision=lax.Precision.HIGHEST, preferred_element_type=F32,
                )
                p = 2 * q + h
                aug[p * N : (p + 1) * N, :] = jnp.where(left, gram + diag, other)
        lane8 = lax.broadcasted_iota(jnp.int32, (patches, 2 * PV), 1)
        for i in range(N):
            rows[i] = aug[pl.ds(i, patches, stride=N), :]
        for k in range(0, N, PIVOTS):
            span = range(PIVOTS)
            top = [rows[k + q] for q in span]
            small = [[jnp.broadcast_to(top[q][:, k + s : k + s + 1], top[q].shape) for s in span] for q in span]
            for q in span:
                inverse = 1.0 / small[q][q]
                top[q] = top[q] * inverse
                small[q] = [x * inverse for x in small[q]]
                for s in span:
                    if s != q:
                        factor = small[s][q]
                        top[s] = top[s] - factor * top[q]
                        small[s] = [x - factor * y for x, y in zip(small[s], small[q])]
            top = [jnp.where(lane8 >= k, x, 0.0) for x in top]
            for q in span:
                rows[k + q] = top[q]
            for i in list(range(k + PIVOTS, N)) + list(range(k)):
                other = rows[i]
                new = other
                for q in span:
                    new = new - other[:, k + q : k + q + 1] * top[q]
                rows[i] = new
        for i in range(N):
            solved[pl.ds(i, patches, stride=N), :] = rows[i]
        for q in range(patches // 2):
            here = slice(q * 2 * PV, (q + 1) * 2 * PV)
            even = solved[2 * q * N : (2 * q + 1) * N, :]
            odd = solved[(2 * q + 1) * N : (2 * q + 2) * N, :]
            both = jnp.where(left, pltpu.roll(even, PV, 1), odd)
            patch, dual = vol[:, here], sd[:, here]
            result = (patch + dual) - SHRINK * both
            split_out[:, here] = result
            dual_out[:, here] = dual + patch - result

    return call(
        body,
        [sds((N, width))] * 2,
        (group, *pieces, scaled_dual),
        [SM] + [VM] * (E + 1),
        [
            pltpu.VMEM((N, width), F32),
            pltpu.VMEM((patches * N, 2 * PV), F32),
            pltpu.VMEM((N, patches, 2 * PV), F32),
            pltpu.VMEM((patches * N, 2 * PV), F32),
        ],
        name="shrink",
    )


def swap(x, axis, size, k):
    return lax.ppermute(x, axis, [(i, i ^ k) for i in range(size)])


def gather(own, n, between=None):
    pieces = [None] * n
    pieces[0] = own
    for j in range(n // 2 - 1, 0, -1):
        pieces[2 * j] = swap(own, "views", n, 2 * j)
    if between is not None:
        pieces[2::2] = [piece + between for piece in pieces[2::2]]
    for j in range(n // 2):
        pieces[2 * j + 1] = swap(pieces[2 * j], "views", n, 1)
    return pieces


def scatter_sum(keep, send, n):
    got = [None] * (n // 2)
    for j in range(n // 2 - 1, -1, -1):
        got[j] = swap(send[j], "views", n, 1)
    parts = [keep[0], got[0]]
    for j in range(n // 2 - 1, 0, -1):
        parts.append(swap(keep[j] + got[j], "views", n, 2 * j))
    return parts


def local(tiles, tile_blocks, ray_counts, sinogram, ray_weights, start, split_target, scaled_dual):
    n, E = lax.axis_size("views"), lax.axis_size("energy")
    C, seg = start.shape
    R, T, rays, vb = tiles.shape
    dims = (n, C, seg, R, T, rays, vb)
    me = group = jnp.stack([lax.axis_index("views"), lax.axis_index("energy")]).astype(jnp.int32)
    live = (lax.broadcasted_iota(jnp.int32, (R, rays), 1) < ray_counts[:, None]).astype(F32)
    scale = ray_weights * live.reshape(1, -1)
    split_target, scaled_dual = split_target[0], scaled_dual[0]

    tt, token = prepare(tiles, me, 8)
    tp = split_target_pieces(split_target, scaled_dual, group, E)
    pieces = gather(start, n, token[0, 0])
    tp = [tp[0]] + [swap(tp[k], "energy", E, k) for k in range(1, E)]
    target = join_target(tp, group)

    out = apply("first", dims, me, tile_blocks, *pieces, tt, scale, sinogram, target)
    parts = scatter_sum(out[: n // 2], out[n // 2 : n], n)
    residual = update_first(parts, start, target)
    volume = start

    d = ad = rr = None
    for it in range(ITERS):
        pieces = gather(residual, n)
        mode = "zero" if it == 0 else ("mid" if it + 1 < ITERS else "last")
        ins = (me, tile_blocks, *pieces, tt, scale)
        if it:
            ins += (d, ad, rr)
        out = apply(mode, dims, *ins)
        if mode == "last":
            scal, d, rr = out
            break
        d, rr, ad = out[n:]
        parts = scatter_sum(out[: n // 2], out[n // 2 : n], n)
        volume, residual = update(parts, volume, residual, d, rr)

    scal = scal + swap(scal, "views", n, 1)
    parts = [scal] + [swap(scal, "views", n, 2 * j) for j in range(n // 2 - 1, 0, -1)]
    volume, vp = finish(parts, volume, d, rr, group, E)
    vp = [vp[0]] + [swap(vp[k], "energy", E, k) for k in range(1, E)]
    new_split, new_dual = shrink(vp, scaled_dual, group)
    return volume, new_split[None], new_dual[None]


def solution(mesh):
    placed = (
        P("views", None, None, None),
        P("views", None),
        P("views"),
        P("energy", "views"),
        P("energy", "views"),
        P("energy", "views"),
        P("views", None, "energy"),
        P("views", None, "energy"),
    )
    return jax.shard_map(
        local,
        mesh=mesh,
        in_specs=placed,
        out_specs=(P("energy", "views"), P("views", None, "energy"), P("views", None, "energy")),
        check_vma=False,
    )
```

```python
import jax
import jax.numpy as jnp
from jax import lax
from jax.experimental import pallas as pl
from jax.experimental.pallas import tpu as pltpu
from jax.sharding import PartitionSpec as P


PV = 64
ITERS = 3
PENALTY = 1.0
SHRINK = 16.0
LANES = 128
LOOPED = ("first", "mid")
PIVOTS = 2
F32, BF16 = jnp.float32, jnp.bfloat16

VM = pl.BlockSpec(memory_space=pltpu.VMEM)
SM = pl.BlockSpec(memory_space=pltpu.SMEM)
ANY = pl.BlockSpec(memory_space=pl.ANY)
MIB = 1 << 20


def sds(shape, dtype=F32):
    return jax.ShapeDtypeStruct(shape, dtype)


def call(body, outs, ins, specs, scratch=(), limit=12, flops=0, moved=0, out_specs=None):
    return pl.pallas_call(
        body,
        out_shape=outs,
        in_specs=specs,
        out_specs=out_specs if out_specs is not None else jax.tree.map(lambda _: VM, outs),
        scratch_shapes=list(scratch),
        compiler_params=pltpu.CompilerParams(vmem_limit_bytes=limit * MIB),
        cost_estimate=pl.CostEstimate(flops=flops, bytes_accessed=moved, transcendentals=0),
    )(*ins)


def halves(x):
    hi = x.astype(BF16).astype(F32)
    return hi, x - hi


def prepare(tiles, ids, step, depth=6):
    R, T, rays, width = tiles.shape
    per = T // step
    trips = R * per

    def body(ids_ref, src, out, buf, sem):
        def copy(i):
            slot = lax.rem(i, depth)
            at = lax.rem(i, per) * step
            return pltpu.make_async_copy(src.at[i // per, pl.ds(at, step)], buf.at[slot], sem.at[slot])

        for a in range(depth - 1):
            copy(a).start()

        def trip(i, carry):
            @pl.when(i + depth - 1 < trips)
            def _():
                copy(i + depth - 1).start()

            copy(i).wait()
            slot = lax.rem(i, depth)
            r, base = i // per, lax.rem(i, per) * step
            for a in range(step):
                hi, lo = halves(buf[slot, a])
                at = pl.multiple_of((base + a) * width, width)
                out[r, :rays, pl.ds(at, width)] = hi.astype(BF16)
                out[r, rays:, pl.ds(at, width)] = lo.astype(BF16)
            return carry

        lax.fori_loop(0, trips, trip, 0)

    return call(
        body,
        pltpu.VMEM((R, 2 * rays, T * width), BF16),
        (ids, tiles),
        [SM, ANY],
        [pltpu.VMEM((depth, step, rays, width), F32), pltpu.SemaphoreType.DMA((depth,))],
        moved=tiles.size * 8,
        flops=tiles.size * 4,
    )


def apply_body(mode, dims, refs):
    n, C, seg, R, T, rays, vb = dims
    nb = seg // vb
    ext = LANES if mode != "first" else 0
    it = iter(refs)
    me_ref, blocks = next(it), next(it)
    pieces = [next(it) for _ in range(n)]
    tt, scale_ref = next(it), next(it)
    if mode == "first":
        sino = next(it)
    if mode in ("mid", "last"):
        d_prev, ad_prev, rr_prev = next(it), next(it), next(it)
    if mode != "last":
        keep = [next(it) for _ in range(n // 2)]
        send = [next(it) for _ in range(n // 2)]
    if mode == "last":
        scal_out = next(it)
    if mode != "first":
        d_out, rr_out = next(it), next(it)
    if mode in ("zero", "mid"):
        ad_out = next(it)
    vs = next(it)
    weighted = next(it)
    columns = next(it)
    acc = next(it) if mode != "last" else None
    me = me_ref[0]

    for i in range(n):
        dev = me ^ i
        for j in range(nb):
            hi, lo = halves(pieces[i][:, j * vb : (j + 1) * vb])
            vs[dev * nb + j] = jnp.concatenate([hi, lo], axis=0).astype(BF16)

    partial = jnp.zeros((C, LANES), F32)
    beta = None
    if mode != "first":
        parts = pieces[0][:, seg:]
        for i in range(1, n):
            parts = parts + pieces[i][:, seg:]
        rr = jnp.sum(parts, axis=1, keepdims=True)
        rr_out[...] = jnp.broadcast_to(rr, (C, LANES))
        d = pieces[0][:, :seg]
        if mode != "zero":
            beta = rr / rr_prev[:, :1]
            d = d + beta * d_prev[...]
        d_out[...] = d
        squares = d * d
        for j in range(seg // LANES):
            partial = partial + squares[:, j * LANES : (j + 1) * LANES]

    for r in range(R):
        for t in range(T):
            columns[:, t * vb : (t + 1) * vb] = vs[blocks[r, t]]
        total = lax.dot_general(
            tt[r], columns[...], (((1,), (1,)), ((), ())), preferred_element_type=F32
        ).T
        both = total[:C] + total[C:]
        ray = both[:, :rays] + both[:, rays:]
        here = slice(r * rays, (r + 1) * rays)
        scale = scale_ref[:, here]
        if mode == "first":
            weight = scale * (sino[:, here] - ray)
        else:
            if mode != "zero":
                ray = ray + beta * ad_prev[:, here]
            if mode != "last":
                ad_out[:, here] = ray
            weight = scale * ray
            product = weight * ray
            for j in range(rays // LANES):
                partial = partial + product[:, j * LANES : (j + 1) * LANES]
        if mode != "last":
            hi, lo = halves(weight)
            stacked = jnp.concatenate([hi, lo], axis=0)
            weighted[r] = jnp.concatenate([stacked, stacked], axis=1).astype(BF16)
    if mode == "last":
        scal_out[...] = partial
        return

    acc[...] = jnp.zeros_like(acc)

    def back(r, carry):
        lhs = weighted[r]

        for t in range(T):
            out = lax.dot_general(
                lhs, tt[r, :, t * vb : (t + 1) * vb], (((1,), (0,)), ((), ())), preferred_element_type=F32
            )
            b = blocks[r, t]
            acc[b] = acc[b] + (out[:C] + out[C:])
        return carry

    if mode in LOOPED:
        lax.fori_loop(0, R, back, 0)
    else:
        for r in range(R):
            back(r, 0)

    for j in range(n // 2):
        for dest, out in ((me ^ (2 * j), keep[j]), (me ^ (2 * j + 1), send[j])):
            for q in range(nb):
                out[:, q * vb : (q + 1) * vb] = acc[dest * nb + q]
            if ext:
                out[:, seg:] = partial


def apply(mode, dims, *ins):
    n, C, seg, R, T, rays, vb = dims
    ext = LANES if mode != "first" else 0
    outs = []
    if mode != "last":
        outs += [sds((C, seg + ext))] * n
    else:
        outs += [sds((C, LANES))]
    if mode != "first":
        outs += [sds((C, seg)), sds((C, LANES))]
    if mode in ("zero", "mid"):
        outs += [sds((C, R * rays))]
    scratch = [
        pltpu.VMEM((n * (seg // vb), 2 * C, vb), BF16),
        pltpu.VMEM((R, 2 * C, 2 * rays), BF16),
        pltpu.VMEM((2 * C, T * vb), BF16),
    ]
    if mode != "last":
        scratch.append(pltpu.VMEM((n * (seg // vb), C, vb), F32))
    specs = [SM, SM] + [VM] * (len(ins) - 2)
    return call(
        lambda *refs: apply_body(mode, dims, refs),
        outs,
        ins,
        specs,
        scratch,
        flops=4 * C * R * T * rays * vb,
        moved=R * T * rays * vb * 4,
    )


def fold(x):
    total = x[:, :LANES]
    for j in range(1, x.shape[1] // LANES):
        total = total + x[:, j * LANES : (j + 1) * LANES]
    return total


def update_first(parts, volume, target):
    C, seg = volume.shape

    def body(*refs):
        got = refs[: len(parts)]
        vol, tgt, out = refs[len(parts) :]
        total = got[0][...]
        for g in got[1:]:
            total = total + g[...]
        r = total + PENALTY * (tgt[...] - vol[...])
        out[:, :seg] = r
        out[:, seg:] = fold(r * r)

    return call(body, sds((C, seg + LANES)), (*parts, volume, target), [VM] * (len(parts) + 2))


def update(parts, volume, residual, direction, rr):
    C, seg = volume.shape

    def body(*refs):
        got = refs[: len(parts)]
        vol, res, dirn, rr_ref, vol_out, out = refs[len(parts) :]
        total = got[0][...]
        for g in got[1:]:
            total = total + g[...]
        d = dirn[...]
        alpha = rr_ref[:, :1] / jnp.sum(total[:, seg:], axis=1, keepdims=True)
        vol_out[...] = vol[...] + alpha * d
        r = res[:, :seg] - alpha * (total[:, :seg] + PENALTY * d)
        out[:, :seg] = r
        out[:, seg:] = fold(r * r)

    return call(
        body,
        [sds((C, seg)), sds((C, seg + LANES))],
        (*parts, volume, residual, direction, rr),
        [VM] * (len(parts) + 4),
    )


def finish(parts, volume, direction, rr, group, E):
    C, seg = volume.shape
    width = seg // E

    def body(*refs):
        e_ref, got = refs[0], refs[1 : 1 + len(parts)]
        vol, dirn, rr_ref, vol_out = refs[1 + len(parts) : 5 + len(parts)]
        outs = refs[5 + len(parts) :]
        total = got[0][...]
        for g in got[1:]:
            total = total + g[...]
        alpha = rr_ref[:, :1] / jnp.sum(total, axis=1, keepdims=True)
        vol_out[...] = vol[...] + alpha * dirn[...]
        for k in range(E):
            at = pl.multiple_of((e_ref[1] ^ k) * width, LANES)
            outs[k][...] = vol_out[:, pl.ds(at, width)]

    got = call(
        body,
        [sds((C, seg))] + [sds((C, width))] * E,
        (group, *parts, volume, direction, rr),
        [SM] + [VM] * (len(parts) + 3),
    )
    return got[0], got[1:]


def split_target_pieces(split_target, scaled_dual, group, E):
    full, width = split_target.shape
    C = full // E

    def body(e_ref, st, sd, *outs):
        for k in range(E):
            at = pl.multiple_of((e_ref[1] ^ k) * C, 8)
            outs[k][...] = st[pl.ds(at, C), :] - sd[pl.ds(at, C), :]

    return call(body, [sds((C, width))] * E, (group, split_target, scaled_dual), [SM, VM, VM])


def join_target(pieces, group):
    E = len(pieces)
    C, width = pieces[0].shape

    def body(e_ref, *refs):
        for k in range(E):
            at = pl.multiple_of((e_ref[1] ^ k) * width, LANES)
            refs[E][:, pl.ds(at, width)] = refs[k][...]

    return call(body, sds((C, width * E)), (group, *pieces), [SM] + [VM] * E)


def shrink(pieces, scaled_dual, group):
    E = len(pieces)
    C, width = pieces[0].shape
    N = C * E
    patches = width // PV

    def body(e_ref, *refs):
        got, sd = refs[:E], refs[E]
        split_out, dual_out, vol, aug, rows, solved = refs[E + 1 :]
        for k in range(E):
            at = pl.multiple_of((e_ref[1] ^ k) * C, 8)
            vol[pl.ds(at, C), :] = got[k][...]
        lane = lax.broadcasted_iota(jnp.int32, (N, 2 * PV), 1)
        left = lane < PV
        diag = jnp.where(lane == lax.broadcasted_iota(jnp.int32, (N, 2 * PV), 0), F32(SHRINK), F32(0))
        for q in range(patches // 2):
            here = slice(q * 2 * PV, (q + 1) * 2 * PV)
            pair = vol[:, here] + sd[:, here]
            turned = pltpu.roll(pair, PV, 1)
            for h, (first, other) in enumerate(((pair, turned), (turned, pair))):
                only = jnp.where(left, first, 0.0)
                gram = lax.dot_general(
                    only, jnp.concatenate([first, first], axis=0), (((1,), (1,)), ((), ())),
                    precision=lax.Precision.HIGHEST, preferred_element_type=F32,
                )
                p = 2 * q + h
                aug[p * N : (p + 1) * N, :] = jnp.where(left, gram + diag, other)
        lane8 = lax.broadcasted_iota(jnp.int32, (patches, 2 * PV), 1)
        for i in range(N):
            rows[i] = aug[pl.ds(i, patches, stride=N), :]
        for k in range(0, N, PIVOTS):
            span = range(PIVOTS)
            top = [rows[k + q] for q in span]
            small = [[jnp.broadcast_to(top[q][:, k + s : k + s + 1], top[q].shape) for s in span] for q in span]
            for q in span:
                inverse = 1.0 / small[q][q]
                top[q] = top[q] * inverse
                small[q] = [x * inverse for x in small[q]]
                for s in span:
                    if s != q:
                        factor = small[s][q]
                        top[s] = top[s] - factor * top[q]
                        small[s] = [x - factor * y for x, y in zip(small[s], small[q])]
            top = [jnp.where(lane8 >= k, x, 0.0) for x in top]
            for q in span:
                rows[k + q] = top[q]
            for i in list(range(k + PIVOTS, N)) + list(range(k)):
                other = rows[i]
                new = other
                for q in span:
                    new = new - other[:, k + q : k + q + 1] * top[q]
                rows[i] = new
        for i in range(N):
            solved[pl.ds(i, patches, stride=N), :] = rows[i]
        for q in range(patches // 2):
            here = slice(q * 2 * PV, (q + 1) * 2 * PV)
            even = solved[2 * q * N : (2 * q + 1) * N, :]
            odd = solved[(2 * q + 1) * N : (2 * q + 2) * N, :]
            both = jnp.where(left, pltpu.roll(even, PV, 1), odd)
            patch, dual = vol[:, here], sd[:, here]
            result = (patch + dual) - SHRINK * both
            split_out[:, here] = result
            dual_out[:, here] = dual + patch - result

    return call(
        body,
        [sds((N, width))] * 2,
        (group, *pieces, scaled_dual),
        [SM] + [VM] * (E + 1),
        [
            pltpu.VMEM((N, width), F32),
            pltpu.VMEM((patches * N, 2 * PV), F32),
            pltpu.VMEM((N, patches, 2 * PV), F32),
            pltpu.VMEM((patches * N, 2 * PV), F32),
        ],
    )


def swap(x, axis, size, k):
    return lax.ppermute(x, axis, [(i, i ^ k) for i in range(size)])


def gather(own, n):
    pieces = [None] * n
    pieces[0] = own
    for j in range(n // 2 - 1, 0, -1):
        pieces[2 * j] = swap(own, "views", n, 2 * j)
    for j in range(n // 2):
        pieces[2 * j + 1] = swap(pieces[2 * j], "views", n, 1)
    return pieces


def scatter_sum(keep, send, n):
    got = [None] * (n // 2)
    for j in range(n // 2 - 1, -1, -1):
        got[j] = swap(send[j], "views", n, 1)
    parts = [keep[0], got[0]]
    for j in range(n // 2 - 1, 0, -1):
        total = keep[j] + got[j]
        parts.append(swap(total, "views", n, 2 * j))
    return parts


def local(tiles, tile_blocks, ray_counts, sinogram, ray_weights, start, split_target, scaled_dual):
    n, E = lax.axis_size("views"), lax.axis_size("energy")
    C, seg = start.shape
    R, T, rays, vb = tiles.shape
    dims = (n, C, seg, R, T, rays, vb)
    me = group = jnp.stack([lax.axis_index("views"), lax.axis_index("energy")]).astype(jnp.int32)
    live = (lax.broadcasted_iota(jnp.int32, (R, rays), 1) < ray_counts[:, None]).astype(F32)
    scale = ray_weights * live.reshape(1, -1)
    split_target, scaled_dual = split_target[0], scaled_dual[0]

    tt = prepare(tiles, me, 8)
    tp = list(split_target_pieces(split_target, scaled_dual, group, E))
    pieces = gather(start, n)
    for k in range(1, E):
        tp[k] = swap(tp[k], "energy", E, k)
    target = join_target(tp, group)

    out = apply("first", dims, me, tile_blocks, *pieces, tt, scale, sinogram)
    parts = scatter_sum(out[: n // 2], out[n // 2 : n], n)
    residual = update_first(parts, start, target)
    volume = start

    d = ad = rr = None
    for it in range(ITERS):
        pieces = gather(residual, n)
        mode = "zero" if it == 0 else ("mid" if it + 1 < ITERS else "last")
        ins = (me, tile_blocks, *pieces, tt, scale)
        if it:
            ins += (d, ad, rr)
        out = apply(mode, dims, *ins)
        if mode == "last":
            scal, d, rr = out
            break
        d, rr, ad = out[n:]
        parts = scatter_sum(out[: n // 2], out[n // 2 : n], n)
        volume, residual = update(parts, volume, residual, d, rr)

    scal = scal + swap(scal, "views", n, 1)
    parts = [scal] + [swap(scal, "views", n, 2 * j) for j in range(n // 2 - 1, 0, -1)]
    volume, vp = finish(parts, volume, d, rr, group, E)
    vp = [vp[0]] + [swap(vp[k], "energy", E, k) for k in range(1, E)]
    new_split, new_dual = shrink(vp, scaled_dual, group)
    return volume, new_split[None], new_dual[None]


def solution(mesh):
    placed = (
        P("views", None, None, None),
        P("views", None),
        P("views"),
        P("energy", "views"),
        P("energy", "views"),
        P("energy", "views"),
        P("views", None, "energy"),
        P("views", None, "energy"),
    )
    return jax.shard_map(
        local,
        mesh=mesh,
        in_specs=placed,
        out_specs=(P("energy", "views"), P("views", None, "energy"), P("views", None, "energy")),
        check_vma=False,
    )
```
